32 devices in a mesh: groups: 2 (over x), mem: 8 (over z, y), tp: 2 (over core).
Axes of the slice: x: 2, y: 2, z: 4, core: 2. Of those that a mesh axis runs over, the one named last changes fastest.
Arguments:
- hidden: bfloat16 [128, 8192], P('groups', 'mem'), parts along dimension 0, may hold values from -6 to 6
- adapter: int32 [128], P('groups'), parts along dimension 0, may hold values from 0 to 31
- page_cache_slot: int32 [256], P('groups'), parts along dimension 0, may hold values from 0 to 127, as said below
- selection: int32 [128, 128], P('groups'), parts along dimension 0, may hold values from 0 to 1, as said below
- query_projection_weight: bfloat16 [8192, 8192], P('mem', 'tp'), may hold values from -0.0625 to 0.0625
- key_projection_weight: bfloat16 [8192, 1024], P('mem', 'tp'), may hold values from -0.0625 to 0.0625
- value_projection_weight: bfloat16 [8192, 1024], P('mem', 'tp'), may hold values from -0.0625 to 0.0625
- adapter_down_weight: bfloat16 [8192, 2048], P('mem'), may hold values from -0.0625 to 0.0625
- adapter_up_weight: bfloat16 [64, 32, 8192], P('mem', None, 'tp'), may hold values from -0.75 to 0.75
- output_projection_weight: bfloat16 [8192, 8192], P('tp', 'mem'), may hold values from -0.0625 to 0.0625
- prefix_key_cache: bfloat16 [256, 128, 1024], P(('groups', 'mem'), None, 'tp'), parts along dimension 0, may hold values from -60 to 60
- prefix_value_cache: bfloat16 [256, 128, 1024], P(('groups', 'mem'), None, 'tp'), parts along dimension 0, may hold values from -6 to 6
Outputs:
- attn_out: bfloat16 [128, 8192], P('groups', 'mem'), parts along dimension 0
The draws below stay inside these ranges and needn't reach their ends.
There are 2 independent parts, one for each index of `groups`. The reference program is written for one: setup_inputs(seed, part) draws one part's arguments, and reference() takes and returns one part's arrays. A program takes and returns all parts, laid end to end along the dimension named above; an argument that names none is the same for every part. Nothing has to cross between parts.
Inputs may be any that keep to these rules, and one draw needn't show every extreme that they name: A permutation: page p is held in cache slot page_cache_slot[p], and slot s lies with index s // 16 of mem. `selection`: every page is selected by 1 to 32 forks; on some index of mem every page held there is selected by exactly 32 forks. A fork may select no page.
All inputs are finite; a program needn't handle non-finite values.
Results may differ from the reference program's by a relative error of at most 0.006.
The reference program's roundings to bfloat16 on the way count: a program that leaves them out, or rounds other values in their place, can miss the bound.
Values may be sent and summed in bfloat16 or wider, within the bound.
A program may use at most 128 MiB of HBM per device.

```python
import math
import jax
import jax.numpy as jnp
import numpy as np
from jax import lax

MODEL_WIDTH = 8192
QUERY_HEADS = 64
KV_HEADS = 8
HEAD_WIDTH = 128
ADAPTER_RANK = 64
ADAPTER_COUNT = 32
PAGE = 128
HOT = 32
PAGE_DEV = 16
FORKS = 64
PAGES = 128


def layout_tables(key):
    base = jax.random.fold_in(key, 4242)
    key_perm, key_count, key_hot, key_rank = jax.random.split(base, 4)
    page_cache_slot = jax.random.permutation(key_perm, PAGES).astype(jnp.int32)
    counts_slot = jax.random.randint(key_count, (PAGES,), 1, HOT + 1)
    devices_count = PAGES // PAGE_DEV
    hot_device = jax.random.randint(key_hot, (), 0, devices_count)
    slot_ids = jnp.arange(PAGES)
    counts_slot = jnp.where(slot_ids // PAGE_DEV == hot_device, HOT, counts_slot)
    counts_page = counts_slot[page_cache_slot]
    fork_orders = jax.vmap(lambda subkey: jax.random.permutation(subkey, FORKS))(jax.random.split(key_rank, PAGES))
    ranking = jnp.argsort(fork_orders, axis=1)
    chosen = (ranking < counts_page[:, None]).astype(jnp.int32)
    return (page_cache_slot, chosen.T)


def draw_page_cache_slot(key, part):
    return layout_tables(key)[0]


def draw_selection(key, part):
    return layout_tables(key)[1]


def draw_prefix_key_cache(key, part):
    key_value = jax.random.fold_in(jax.random.fold_in(key, 77), 1)
    raw = jax.random.normal(key_value, (PAGES, PAGE, KV_HEADS * HEAD_WIDTH))
    return jnp.clip(raw, -6.0, 6.0).astype(jnp.bfloat16)


def with_ends(array, own_key, smallest, high):
    dims = array.shape
    spot = [jax.random.randint(jax.random.fold_in(own_key, axis), (), 0, dims[axis]) for axis in range(len(dims))]
    array = array.at[tuple(spot)].set(smallest)
    longest = dims.index(max(dims))
    spot[longest] = (spot[longest] + 1) % dims[longest]
    return array.at[tuple(spot)].set(high)


def block_scale(rng, shape, pieces, least, high):
    level = 1.0
    for dim, blocks in pieces:
        steps = jax.random.uniform(jax.random.fold_in(jax.random.fold_in(rng, 6), dim), (blocks,), jnp.float32, least / len(pieces), high / len(pieces))
        level = level * jnp.repeat(jnp.exp(steps), shape[dim] // blocks).reshape((-1,) + (1,) * (len(shape) - 1 - dim))
    return level


def rank_table(amount, skew):
    loads = [(1 << 20) // math.isqrt(standing ** skew) + 1 for standing in range(1, amount + 1)]
    scale = 1 + sum(loads) // (1 << 30)
    return np.cumsum(np.array([max(1, weight // scale) for weight in loads]))


def skewed_ids(stream_key, dims, number_of, skew):
    table = rank_table(number_of, skew)
    ticket = jax.random.randint(jax.random.fold_in(stream_key, 1), dims, 0, int(table[number_of - 1]))
    rank = jnp.searchsorted(jnp.asarray(table, jnp.int32), ticket, side="right")
    return jax.random.permutation(jax.random.fold_in(stream_key, 2), number_of)[rank].astype(jnp.int32)


def normal_values(key, extent, width, bound, pieces=(), kind=jnp.bfloat16):
    entries = width * jax.random.normal(key, extent, jnp.float32)
    if pieces:
        entries = entries * block_scale(key, extent, pieces, -0.22, 0.18)
    return jnp.clip(entries, -bound, bound).astype(kind)


def setup_inputs(seed: int = 0, part: int = 0) -> dict:
    key_of = jax.random.split(jax.random.key(seed), 13)
    part_keys = jax.random.split(jax.random.fold_in(key_of[12], part), 13)
    return {
        "hidden": normal_values(part_keys[0], (FORKS, MODEL_WIDTH), 1.0, 6.0, ((1, 8),)),
        "adapter": with_ends(skewed_ids(part_keys[1], (FORKS,), ADAPTER_COUNT, 2), jax.random.fold_in(part_keys[1], 3), 0, ADAPTER_COUNT - 1).astype(jnp.int32),
        "page_cache_slot": draw_page_cache_slot(jax.random.fold_in(jax.random.fold_in(key_of[12], part), 71), part),
        "selection": draw_selection(jax.random.fold_in(jax.random.fold_in(key_of[12], part), 71), part),
        "query_projection_weight": normal_values(key_of[4], (MODEL_WIDTH, QUERY_HEADS * HEAD_WIDTH), MODEL_WIDTH ** -0.5, 0.0625, ((0, 8), (1, 2))),
        "key_projection_weight": normal_values(key_of[5], (MODEL_WIDTH, KV_HEADS * HEAD_WIDTH), MODEL_WIDTH ** -0.5, 0.0625, ((0, 8), (1, 2))),
        "value_projection_weight": normal_values(key_of[6], (MODEL_WIDTH, KV_HEADS * HEAD_WIDTH), MODEL_WIDTH ** -0.5, 0.0625, ((0, 8), (1, 2))),
        "adapter_down_weight": normal_values(key_of[7], (MODEL_WIDTH, ADAPTER_COUNT * ADAPTER_RANK), MODEL_WIDTH ** -0.5, 0.0625, ((0, 8),)),
        "adapter_up_weight": normal_values(key_of[8], (ADAPTER_RANK, ADAPTER_COUNT, QUERY_HEADS * HEAD_WIDTH), ADAPTER_RANK ** -0.5, 0.75, ((0, 8), (2, 2))),
        "output_projection_weight": normal_values(key_of[9], (QUERY_HEADS * HEAD_WIDTH, MODEL_WIDTH), (QUERY_HEADS * HEAD_WIDTH) ** -0.5, 0.0625, ((0, 2), (1, 8))),
        "prefix_key_cache": draw_prefix_key_cache(jax.random.fold_in(jax.random.fold_in(key_of[12], part), 71), part),
        "prefix_value_cache": normal_values(part_keys[11], (PAGES, PAGE, KV_HEADS * HEAD_WIDTH), 1.0, 6.0, ((0, 8), (2, 2))),
    }


adapter_scale = 1.0
neg_floor = -1e30


def reference(hidden, adapter, page_cache_slot, selection, query_projection_weight, key_projection_weight, value_projection_weight, adapter_down_weight, adapter_up_weight, output_projection_weight, prefix_key_cache, prefix_value_cache):
    every_fork_list = hidden.shape[0]
    group_size = QUERY_HEADS // KV_HEADS
    score_scale = HEAD_WIDTH ** -0.5
    onehot = (adapter[:, None] == jnp.arange(ADAPTER_COUNT, dtype=jnp.int32)[None, :]).astype(jnp.float32)
    down_activations = jnp.dot(hidden, adapter_down_weight, preferred_element_type=jnp.float32).reshape(every_fork_list, ADAPTER_COUNT, ADAPTER_RANK)
    rank_acts = jnp.sum(down_activations * onehot[:, None, :].transpose(0, 2, 1), axis=1).astype(jnp.bfloat16)
    spread_factor = (rank_acts.astype(jnp.float32)[:, :, None] * onehot[:, None, :]).astype(jnp.bfloat16)
    spread_factor = spread_factor.reshape(every_fork_list, ADAPTER_RANK * ADAPTER_COUNT)
    adapter_query_delta = jnp.dot(spread_factor, adapter_up_weight.reshape(ADAPTER_RANK * ADAPTER_COUNT, QUERY_HEADS * HEAD_WIDTH), preferred_element_type=jnp.float32)
    query_vectors = (jnp.dot(hidden, query_projection_weight, preferred_element_type=jnp.float32) + adapter_scale * adapter_query_delta).astype(jnp.bfloat16)
    key_new = jnp.dot(hidden, key_projection_weight, preferred_element_type=jnp.float32).astype(jnp.bfloat16)
    value_new = jnp.dot(hidden, value_projection_weight, preferred_element_type=jnp.float32).astype(jnp.bfloat16)
    page_total = page_cache_slot.shape[0]
    page_of_slot = jnp.zeros((page_total,), jnp.int32).at[page_cache_slot].set(jnp.arange(page_total, dtype=jnp.int32))
    query_pad = jnp.concatenate([query_vectors, jnp.zeros((1, QUERY_HEADS * HEAD_WIDTH), jnp.bfloat16)], axis=0)
    query_pad = query_pad.reshape(every_fork_list + 1, KV_HEADS, group_size, HEAD_WIDTH)

    def visit(state_now, scan_items):
        maxima, totals, summed = state_now
        page_keys, page_values, page_id = scan_items
        column = jnp.take(selection, page_id, axis=1)
        chosen = jnp.nonzero(column > 0, size=HOT, fill_value=every_fork_list)[0].astype(jnp.int32)
        picked = query_pad[chosen].astype(jnp.float32)
        keys_f = page_keys.reshape(PAGE, KV_HEADS, HEAD_WIDTH).astype(jnp.float32)
        values_f = page_values.reshape(PAGE, KV_HEADS, HEAD_WIDTH).astype(jnp.float32)
        scores = jnp.einsum('hkgd,tkd->hkgt', picked, keys_f) * score_scale
        page_peak = jnp.max(scores, axis=-1)
        weights = jnp.exp(scores - page_peak[..., None]).astype(jnp.bfloat16).astype(jnp.float32)
        masses = jnp.sum(weights, axis=-1)
        partial_value = jnp.einsum('hkgt,tkd->hkgd', weights, values_f)
        old_max = maxima[chosen]
        new_max = jnp.maximum(old_max, page_peak)
        keep_old = jnp.exp(old_max - new_max)
        fresh_w = jnp.exp(page_peak - new_max)
        totals = totals.at[chosen].set(totals[chosen] * keep_old + masses * fresh_w)
        summed = summed.at[chosen].set(summed[chosen] * keep_old[..., None] + partial_value * fresh_w[..., None])
        maxima = maxima.at[chosen].set(new_max)
        return (maxima, totals, summed), None

    start_state = (jnp.full((every_fork_list + 1, KV_HEADS, group_size), neg_floor, jnp.float32),
                   jnp.zeros((every_fork_list + 1, KV_HEADS, group_size), jnp.float32),
                   jnp.zeros((every_fork_list + 1, KV_HEADS, group_size, HEAD_WIDTH), jnp.float32))
    final_state, unused = lax.scan(visit, start_state, (prefix_key_cache, prefix_value_cache, page_of_slot))
    maxima = final_state[0][:every_fork_list]
    totals = final_state[1][:every_fork_list]
    summed = final_state[2][:every_fork_list]
    query_f = query_vectors.reshape(every_fork_list, KV_HEADS, group_size, HEAD_WIDTH).astype(jnp.float32)
    key_f = key_new.reshape(every_fork_list, KV_HEADS, 1, HEAD_WIDTH).astype(jnp.float32)
    value_f = value_new.reshape(every_fork_list, KV_HEADS, 1, HEAD_WIDTH).astype(jnp.float32)
    own_score = jnp.sum(query_f * key_f, axis=-1) * score_scale
    final_max = jnp.maximum(maxima, own_score)
    old_weight = jnp.exp(maxima - final_max)
    own_weight = jnp.exp(own_score - final_max)
    normalized = (summed * old_weight[..., None] + own_weight[..., None] * value_f) / (totals * old_weight + own_weight)[..., None]
    attended = normalized.astype(jnp.bfloat16).reshape(every_fork_list, QUERY_HEADS * HEAD_WIDTH)
    return jnp.dot(attended, output_projection_weight, preferred_element_type=jnp.float32).astype(jnp.bfloat16)
```

```python
import functools
import math

import jax
import jax.numpy as jnp
from jax import lax
from jax.experimental import pallas as pl
from jax.experimental.pallas import tpu as pltpu
from jax.sharding import PartitionSpec as P

HEAD_WIDTH = 128
ADAPTER_RANK = 64
ADAPTER_COUNT = 32
MESH = pl.DeviceIdType.MESH
F32 = jnp.float32
BF16 = jnp.bfloat16
neg_floor = -1e30


def dot(x, y, dims=((1,), (0,))):
    return lax.dot_general(x, y, (dims, ((), ())), preferred_element_type=F32)


def kernel(
    n,
    group_size,
    hidden,
    adapter,
    slots,
    selection,
    wq,
    wk,
    wv,
    down,
    up,
    wo,
    kcache,
    vcache,
    out,
    dbuf,
    kvbuf,
    wqbuf,
    upbuf,
    kbuf,
    vbuf,
    wobuf,
    rtx,
    rrx,
    kvp,
    part,
    rx1,
    tx2,
    rx2,
    qfull,
    kvx,
    selx,
    acc,
    stat,
    resa,
    ress,
    rxa,
    rxs,
    txa,
    txs,
    fxa,
    fxs,
    cfull,
    outp,
    outr,
    loc,
    rsend,
    rrecv,
    s1,
    r1,
    s2,
    r2,
    ksem,
    gs,
    gr,
    hs,
    hr,
    as1,
    ar1,
    bs1,
    br1,
    as2,
    ar2,
    bs2,
    br2,
    osem,
):
    half = n // 2
    me = lax.axis_index("mem")
    core = lax.axis_index("tp")
    a = me // 2
    b = me % 2
    forks = hidden.shape[0]
    head_columns = wq.shape[1] // n
    per_owner = head_columns // HEAD_WIDTH
    wide = 2 * head_columns
    lanes = per_owner * forks
    both = 2 * lanes
    kv_local = wk.shape[1] // HEAD_WIDTH
    rank_local = up.shape[0]
    pages = kcache.shape[0]
    tokens = kcache.shape[1]
    sends = []

    def send(src, dst, ssem, rsem, where):
        copy = pltpu.make_async_remote_copy(
            src_ref=src,
            dst_ref=dst,
            send_sem=ssem,
            recv_sem=rsem,
            device_id=where,
            device_id_type=MESH,
        )
        copy.start()
        sends.append(copy)
        return copy

    def mate():
        return {"mem": me + 1 - 2 * b}

    def far(step):
        return {"mem": 2 * ((a + step) % half) + b}

    order = sorted(range(1, half), key=lambda d: -min(d, half - d)) + [0]
    locals_ = []

    def fetch(src, dst):
        copy = pltpu.make_async_copy(src, dst, loc.at[len(locals_)])
        copy.start()
        locals_.append(copy)
        return copy

    dchunks = dbuf.shape[0]
    dwide = dbuf.shape[2]
    get_down = [fetch(down.at[:, pl.ds(c * dwide, dwide)], dbuf.at[c]) for c in range(dchunks)]
    get_k = fetch(wk, kvbuf.at[0])
    get_v = fetch(wv, kvbuf.at[1])
    get_q, get_up = [], []
    for i, d in enumerate(order):
        columns = pl.ds(pl.multiple_of(((a + d) % half) * wide, wide), wide)
        get_q.append(fetch(wq.at[:, columns], wqbuf.at[i]))
        get_up.append(fetch(up.at[:, :, columns], upbuf.at[i]))
    get_kc = fetch(kcache, kbuf)
    get_vc = fetch(vcache, vbuf)
    get_wo = fetch(wo, wobuf)

    barrier = pltpu.get_barrier_semaphore()
    for o in range(1, n):
        pl.semaphore_signal(barrier, inc=1, device_id={"mem": (me + o) % n}, device_id_type=MESH)
    pl.semaphore_signal(barrier, inc=1, device_id={"tp": 1 - core}, device_id_type=MESH)

    h = hidden[...]
    ids = adapter[...].astype(F32)
    eye = lax.broadcasted_iota(jnp.int32, (forks, forks), 0) == lax.broadcasted_iota(
        jnp.int32, (forks, forks), 1
    )
    id_column = jnp.sum(jnp.where(eye, ids, 0.0), axis=1, keepdims=True)
    per_tile = 128 // ADAPTER_RANK
    lane_part = (
        lax.broadcasted_iota(jnp.int32, (forks, 128), 1) // ADAPTER_RANK
    ).astype(F32)
    folded = jnp.zeros((forks, 128), F32)
    for c in range(dchunks):
        get_down[c].wait()
        act = dot(h, dbuf[c])
        for t in range(dwide // 128):
            first = (c * (dwide // 128) + t) * per_tile
            folded += jnp.where(
                id_column - float(first) == lane_part, act[:, t * 128 : (t + 1) * 128], 0.0
            )
    turned = jnp.transpose(folded)
    rank_part = turned[:ADAPTER_RANK]
    for t in range(1, per_tile):
        rank_part += turned[t * ADAPTER_RANK : (t + 1) * ADAPTER_RANK]
    for j in range(n):
        rtx[j] = rank_part[j * rank_local : (j + 1) * rank_local]
    pl.semaphore_wait(barrier, n)
    rank_moves = []
    for o in range(1, n):
        to = (me + o) % n
        rank_moves.append(
            send(rtx.at[to], rrx.at[o], rsend.at[o], rrecv.at[o], {"mem": to})
        )

    get_k.wait()
    kp = dot(h, kvbuf[0])
    get_v.wait()
    vp = dot(h, kvbuf[1])
    for k in range(kv_local):
        kvp[0, k] = kp[:, k * HEAD_WIDTH : (k + 1) * HEAD_WIDTH]
        kvp[1, k] = vp[:, k * HEAD_WIDTH : (k + 1) * HEAD_WIDTH]

    slot_ids = me * pages + lax.broadcasted_iota(jnp.int32, (pages, slots.shape[1]), 0)
    match = (slots[...] == slot_ids).astype(F32).astype(BF16)
    chosen = dot(match, selection[...].astype(F32).astype(BF16), ((1,), (1,)))
    spread_eye = (
        lax.broadcasted_iota(jnp.int32, (forks, both), 1) % forks
        == lax.broadcasted_iota(jnp.int32, (forks, both), 0)
    ).astype(F32)
    spread_bf = spread_eye.astype(BF16)
    selx[...] = dot(chosen.astype(BF16), spread_bf)

    def kv_of(group):
        return (group * 2 * per_owner) // group_size

    get_q[0].wait()
    base = dot(h, wqbuf[0])
    for move in rank_moves:
        move.wait_recv()
    ranks = rtx[me]
    for o in range(1, n):
        ranks = ranks + rrx[o]
    ranks = ranks.astype(BF16).astype(F32)
    is_adapter = (
        lax.broadcasted_iota(jnp.int32, (ADAPTER_COUNT, forks), 0) == adapter[...]
    )
    rows = [
        jnp.where(is_adapter, ranks[r : r + 1], 0.0) for r in range(rank_local)
    ]
    spread = jnp.transpose(jnp.concatenate(rows, axis=0)).astype(BF16)

    moves1 = []
    for i, d in enumerate(order):
        if i:
            get_q[i].wait()
            base = dot(h, wqbuf[i])
        get_up[i].wait()
        total = base + dot(spread, upbuf[i].reshape(rank_local * ADAPTER_COUNT, wide))
        kv = kv_of((a + d) % half)
        for s in range(2):
            part[i, s, :, :head_columns] = total[:, s * head_columns : (s + 1) * head_columns]
            part[i, s, :, head_columns:] = kvp[s, kv]
        moves1.append(send(part.at[i, 1 - b], rx1.at[i], s1.at[i], r1.at[i], mate()))
    moves2 = []
    for i, d in enumerate(order):
        moves1[i].wait_recv()
        merged = part[i, b] + rx1[i]
        if d:
            tx2[i] = merged
            moves2.append(send(tx2.at[i], rx2.at[d], s2.at[d], r2.at[d], far(d)))
    for i, d in enumerate(order[:-1]):
        moves2[i].wait_recv()
        merged = merged + rx2[d]

    qfull[me] = merged[:, :head_columns].astype(BF16)
    kvx[b] = merged[:, head_columns:].astype(BF16)

    def gather(buf, ssem, rsem):
        near = send(buf.at[me], buf.at[me], ssem.at[0], rsem.at[0], mate())
        z = [
            send(buf.at[me], buf.at[me], ssem.at[d], rsem.at[d], far(d))
            for d in range(1, half)
        ]
        return near, z

    def forward(buf, ssem, rsem, z):
        passed = []
        for d in range(1, half):
            z[d - 1].wait_recv()
            slot = 2 * ((a + half - d) % half) + b
            passed.append(
                send(
                    buf.at[slot],
                    buf.at[slot],
                    ssem.at[half + d - 1],
                    rsem.at[half + d - 1],
                    mate(),
                )
            )
        return passed

    near, z = gather(qfull, gs, gr)
    kv_move = send(kvx.at[b], kvx.at[b], ksem.at[0], ksem.at[1], mate())

    scale = HEAD_WIDTH ** (-0.5)
    scale2 = scale * math.log2(math.e)

    def attend(j, group):
        kv = kv_of(group)
        columns = pl.ds(pl.multiple_of(kv * HEAD_WIDTH, HEAD_WIDTH), HEAD_WIDTH)
        pieces = []
        for s in range(2):
            for t in range(per_owner):
                pieces.append(qfull[2 * group + s, :, t * HEAD_WIDTH : (t + 1) * HEAD_WIDTH])
        queries = jnp.concatenate(pieces, axis=0)
        acc[...] = jnp.zeros_like(acc)
        top0 = jnp.full((1, both), neg_floor, F32)
        mass0 = jnp.zeros((1, both), F32)

        def page(p, carry):
            top, mass = carry
            keys = kbuf[p, :, columns]
            values = vbuf[p, :, columns]
            raw = dot(keys, queries, ((1,), (1,)))
            peak = jnp.max(raw, axis=0, keepdims=True)
            probs = jnp.exp2((raw - peak) * scale2).astype(BF16)
            page_mass = jnp.sum(probs.astype(F32), axis=0, keepdims=True)
            page_acc = dot(values, probs, ((0,), (0,)))
            hit = selx[pl.ds(p, 1), :] > 0.5
            peak = jnp.where(hit, peak, neg_floor)
            new_top = jnp.maximum(top, peak)
            fresh = jnp.where(hit, jnp.exp2((peak - new_top) * scale2), 0.0)
            keep = jnp.exp2((top - new_top) * scale2)
            acc[...] = acc[...] * keep + page_acc * fresh
            return new_top, mass * keep + page_mass * fresh

        top, mass = lax.fori_loop(0, pages, page, (top0, mass0), unroll=2)
        for s in range(2):
            part_lanes = slice(s * lanes, (s + 1) * lanes)
            resa[j, s] = acc[:, part_lanes].astype(BF16)
            ress[j, s, 0:1] = top[:, part_lanes]
            ress[j, s, 1:2] = mass[:, part_lanes]

    def join(items):
        top = items[0][1]
        for item in items[1:]:
            top = jnp.maximum(top, item[1])
        mass, total = 0.0, 0.0
        for x, t, w in items:
            factor = jnp.exp2((t - top) * scale2)
            mass = mass + w * factor
            total = total + x.astype(F32) * factor
        return total, top, mass

    moves3, moves4 = [], []

    def send_half(j):
        moves3.append(
            (
                send(resa.at[j, 1 - b], rxa.at[j], as1.at[j], ar1.at[j], mate()),
                send(ress.at[j, 1 - b], rxs.at[j], bs1.at[j], br1.at[j], mate()),
            )
        )

    def merge_half(j):
        for move in moves3[j]:
            move.wait_recv()
        total, top, mass = join(
            [
                (resa[j, b], ress[j, b, 0:1], ress[j, b, 1:2]),
                (rxa[j], rxs[j, 0:1], rxs[j, 1:2]),
            ]
        )
        if j == 0:
            return total, top, mass
        d = half - j
        txa[j] = total.astype(BF16)
        txs[j, 0:1] = top
        txs[j, 1:2] = mass
        moves4.append(
            (
                d,
                send(txa.at[j], fxa.at[d], as2.at[d], ar2.at[d], far(d)),
                send(txs.at[j], fxs.at[d], bs2.at[d], br2.at[d], far(d)),
            )
        )
        return None

    get_kc.wait()
    get_vc.wait()
    near.wait_recv()
    own_items = None
    passed = None
    for j in range(half):
        if j == 1:
            passed = forward(qfull, gs, gr, z)
        if j:
            passed[j - 1].wait_recv()
        attend(j, (a + half - j) % half)
        send_half(j)
        if j:
            result = merge_half(j - 1)
            if j == 1:
                own_items = result
    last = merge_half(half - 1)
    if half == 1:
        own_items = last

    kv_move.wait_recv()
    mine = jnp.concatenate(
        [qfull[me, :, t * HEAD_WIDTH : (t + 1) * HEAD_WIDTH] for t in range(per_owner)], axis=0
    )
    cross = dot(kvx[0], mine, ((1,), (1,)))
    own_eye = spread_eye[:, :lanes]
    own_score = jnp.sum(jnp.where(own_eye > 0.5, cross, 0.0), axis=0, keepdims=True)
    own_value = dot(kvx[1], own_eye.astype(BF16), ((0,), (0,)))
    items = [own_items, (own_value, own_score, jnp.ones((1, lanes), F32))]
    for d, move_a, move_s in moves4:
        move_a.wait_recv()
        move_s.wait_recv()
        items.append((fxa[d], fxs[d, 0:1], fxs[d, 1:2]))
    total, top, mass = join(items)
    context = jnp.transpose(total / mass)
    for t in range(per_owner):
        cfull[me, :, t * HEAD_WIDTH : (t + 1) * HEAD_WIDTH] = context[
            t * forks : (t + 1) * forks
        ].astype(BF16)

    near, z = gather(cfull, hs, hr)
    get_wo.wait()

    def project(slot):
        rows_ = pl.ds(pl.multiple_of(slot * head_columns, head_columns), head_columns)
        return dot(cfull[slot], wobuf[rows_, :])

    outp[...] = project(me)
    near.wait_recv()
    outp[...] += project(me + 1 - 2 * b)
    passed = forward(cfull, hs, hr, z)
    for d in range(1, half):
        outp[...] += project(2 * ((a + half - d) % half) + b)
    for d in range(1, half):
        passed[d - 1].wait_recv()
        outp[...] += project(2 * ((a + half - d) % half) + 1 - b)
    swap = send(outp, outr, osem.at[0], osem.at[1], {"tp": 1 - core})
    swap.wait_recv()
    out[...] = (outp[...] + outr[...]).astype(out.dtype)
    for copy in sends:
        copy.wait_send()


def shards(
    hidden,
    adapter,
    page_cache_slot,
    selection,
    query_projection_weight,
    key_projection_weight,
    value_projection_weight,
    adapter_down_weight,
    adapter_up_weight,
    output_projection_weight,
    prefix_key_cache,
    prefix_value_cache,
):
    n = lax.axis_size("mem")
    half = n // 2
    forks, depth = hidden.shape
    width = query_projection_weight.shape[1]
    kv_width = key_projection_weight.shape[1]
    kv_local = kv_width // HEAD_WIDTH
    group_size = width // kv_width
    columns = width // n
    lanes = (columns // HEAD_WIDTH) * forks
    out_width = output_projection_weight.shape[1]
    rank_local = adapter_up_weight.shape[0]
    pages, tokens = prefix_key_cache.shape[:2]
    down_width = adapter_down_weight.shape[1]
    chunks = 4
    dma = pltpu.SemaphoreType.DMA
    vmem = pltpu.VMEM
    scratch = [
        vmem((chunks, depth, down_width // chunks), BF16),
        vmem((2, depth, kv_width), BF16),
        vmem((half, depth, 2 * columns), BF16),
        vmem((half, rank_local, ADAPTER_COUNT, 2 * columns), BF16),
        vmem(prefix_key_cache.shape, BF16),
        vmem(prefix_value_cache.shape, BF16),
        vmem(output_projection_weight.shape, BF16),
        vmem((n, rank_local, forks), F32),
        vmem((n, rank_local, forks), F32),
        vmem((2, kv_local, forks, HEAD_WIDTH), F32),
        vmem((half, 2, forks, columns + HEAD_WIDTH), F32),
        vmem((half, forks, columns + HEAD_WIDTH), F32),
        vmem((half, forks, columns + HEAD_WIDTH), F32),
        vmem((half, forks, columns + HEAD_WIDTH), F32),
        vmem((n, forks, columns), BF16),
        vmem((2, forks, HEAD_WIDTH), BF16),
        vmem((pages, 2 * lanes), F32),
        vmem((HEAD_WIDTH, 2 * lanes), F32),
        vmem((8, 2 * lanes), F32),
        vmem((half, 2, HEAD_WIDTH, lanes), BF16),
        vmem((half, 2, 2, lanes), F32),
        vmem((half, HEAD_WIDTH, lanes), BF16),
        vmem((half, 2, lanes), F32),
        vmem((half, HEAD_WIDTH, lanes), BF16),
        vmem((half, 2, lanes), F32),
        vmem((half, HEAD_WIDTH, lanes), BF16),
        vmem((half, 2, lanes), F32),
        vmem((n, forks, columns), BF16),
        vmem((forks, out_width), F32),
        vmem((forks, out_width), F32),
        dma((chunks + 2 + 2 * half + 3,)),
        dma((n,)),
        dma((n,)),
        dma((half,)),
        dma((half,)),
        dma((half,)),
        dma((half,)),
        dma((2,)),
        dma((n,)),
        dma((n,)),
        dma((n,)),
        dma((n,)),
        dma((half,)),
        dma((half,)),
        dma((half,)),
        dma((half,)),
        dma((half,)),
        dma((half,)),
        dma((half,)),
        dma((half,)),
        dma((2,)),
    ]
    small = pl.BlockSpec(memory_space=pltpu.VMEM)
    large = pl.BlockSpec(memory_space=pl.ANY)
    return pl.pallas_call(
        functools.partial(kernel, n, group_size),
        out_shape=jax.ShapeDtypeStruct((forks, out_width), BF16),
        in_specs=[small] * 4 + [large] * 8,
        out_specs=small,
        scratch_shapes=scratch,
        compiler_params=pltpu.CompilerParams(
            collective_id=0, has_side_effects=True, vmem_limit_bytes=60 * 1024 * 1024
        ),
    )(
        hidden,
        adapter.reshape(1, forks),
        page_cache_slot.reshape(1, page_cache_slot.shape[0]),
        selection,
        query_projection_weight,
        key_projection_weight,
        value_projection_weight,
        adapter_down_weight,
        adapter_up_weight,
        output_projection_weight,
        prefix_key_cache,
        prefix_value_cache,
    )


def solution(mesh):
    return jax.shard_map(
        shards,
        mesh=mesh,
        in_specs=(
            P("groups", "mem"),
            P("groups"),
            P("groups"),
            P("groups", None),
            P("mem", "tp"),
            P("mem", "tp"),
            P("mem", "tp"),
            P("mem", None),
            P("mem", None, "tp"),
            P("tp", "mem"),
            P(("groups", "mem"), None, "tp"),
            P(("groups", "mem"), None, "tp"),
        ),
        out_specs=P("groups", "mem"),
        check_vma=False,
    )
```

```python
import functools
import math

import jax
import jax.numpy as jnp
from jax import lax
from jax.experimental import pallas as pl
from jax.experimental.pallas import tpu as pltpu
from jax.sharding import PartitionSpec as P

HEAD_WIDTH = 128
ADAPTER_RANK = 64
ADAPTER_COUNT = 32
MESH = pl.DeviceIdType.MESH
F32 = jnp.float32
BF16 = jnp.bfloat16
neg_floor = -1e30


def dot(x, y, dims=((1,), (0,))):
    return lax.dot_general(x, y, (dims, ((), ())), preferred_element_type=F32)


def kernel(
    n,
    group_size,
    hidden,
    adapter,
    slots,
    selection,
    wq,
    wk,
    wv,
    down,
    up,
    wo,
    kcache,
    vcache,
    out,
    dbuf,
    kvbuf,
    wqbuf,
    upbuf,
    kbuf,
    vbuf,
    vtbuf,
    wobuf,
    rtx,
    rrx,
    kvp,
    kpart,
    krx,
    part,
    rx1,
    tx2,
    rx2,
    qfull,
    kvx,
    selx,
    acc,
    resa,
    ress,
    rxa,
    rxs,
    txa,
    txs,
    fxa,
    fxs,
    cfull,
    outp,
    outr,
    loc,
    rsend,
    rrecv,
    s1,
    r1,
    s2,
    r2,
    ksem,
    gs,
    gr,
    hs,
    hr,
    as1,
    ar1,
    bs1,
    br1,
    as2,
    ar2,
    bs2,
    br2,
    osem,
):
    half = n // 2
    me = lax.axis_index("mem")
    core = lax.axis_index("tp")
    a = me // 2
    b = me % 2
    forks = hidden.shape[0]
    head_columns = wq.shape[1] // n
    per_owner = head_columns // HEAD_WIDTH
    wide = 2 * head_columns
    lanes = per_owner * forks
    both = 2 * lanes
    kv_local = wk.shape[1] // HEAD_WIDTH
    rank_local = up.shape[0]
    pages = kcache.shape[0]
    tokens = kcache.shape[1]
    sends = []

    def send(src, dst, ssem, rsem, where):
        copy = pltpu.make_async_remote_copy(
            src_ref=src,
            dst_ref=dst,
            send_sem=ssem,
            recv_sem=rsem,
            device_id=where,
            device_id_type=MESH,
        )
        copy.start()
        sends.append(copy)
        return copy

    def mate():
        return {"mem": me + 1 - 2 * b}

    def far(step):
        return {"mem": 2 * ((a + step) % half) + b}

    order = sorted(range(1, half), key=lambda d: -min(d, half - d)) + [0]
    locals_ = []

    def fetch(src, dst):
        copy = pltpu.make_async_copy(src, dst, loc.at[len(locals_)])
        copy.start()
        locals_.append(copy)
        return copy

    dchunks = dbuf.shape[0]
    dwide = dbuf.shape[2]
    get_down = [fetch(down.at[:, pl.ds(c * dwide, dwide)], dbuf.at[c]) for c in range(dchunks)]
    get_k = fetch(wk, kvbuf.at[0])
    get_v = fetch(wv, kvbuf.at[1])
    get_q, get_up = [], []

    def fetch_piece(i):
        columns = pl.ds(pl.multiple_of(((a + order[i]) % half) * wide, wide), wide)
        get_q.append(fetch(wq.at[:, columns], wqbuf.at[i]))
        get_up.append(fetch(up.at[:, :, columns], upbuf.at[i]))

    fetch_piece(0)

    barrier = pltpu.get_barrier_semaphore()
    for o in range(1, n):
        pl.semaphore_signal(barrier, inc=1, device_id={"mem": (me + o) % n}, device_id_type=MESH)
    pl.semaphore_signal(barrier, inc=1, device_id={"tp": 1 - core}, device_id_type=MESH)

    h = hidden[...]
    ids = adapter[...].astype(F32)
    eye = lax.broadcasted_iota(jnp.int32, (forks, forks), 0) == lax.broadcasted_iota(
        jnp.int32, (forks, forks), 1
    )
    id_column = jnp.sum(jnp.where(eye, ids, 0.0), axis=1, keepdims=True)
    per_tile = 128 // ADAPTER_RANK
    lane_part = (
        lax.broadcasted_iota(jnp.int32, (forks, 128), 1) // ADAPTER_RANK
    ).astype(F32)
    folded = jnp.zeros((forks, 128), F32)
    for c in range(dchunks):
        get_down[c].wait()
        act = dot(h, dbuf[c])
        for t in range(dwide // 128):
            first = (c * (dwide // 128) + t) * per_tile
            folded += jnp.where(
                id_column - float(first) == lane_part, act[:, t * 128 : (t + 1) * 128], 0.0
            )
    for i in range(1, half):
        fetch_piece(i)
    turned = jnp.transpose(folded)
    rank_part = turned[:ADAPTER_RANK]
    for t in range(1, per_tile):
        rank_part += turned[t * ADAPTER_RANK : (t + 1) * ADAPTER_RANK]
    for j in range(n):
        rtx[j] = rank_part[j * rank_local : (j + 1) * rank_local]
    pl.semaphore_wait(barrier, n)
    rank_moves = []
    for o in range(1, n):
        to = (me + o) % n
        rank_moves.append(
            send(rtx.at[to], rrx.at[o], rsend.at[o], rrecv.at[o], {"mem": to})
        )

    def kv_of(group):
        return (group * 2 * per_owner) // group_size

    get_k.wait()
    kp = dot(h, kvbuf[0])
    get_v.wait()
    vp = dot(h, kvbuf[1])
    get_vc = fetch(vcache, vbuf)
    get_kc = fetch(kcache, kbuf)
    for k in range(kv_local):
        kvp[0, k] = kp[:, k * HEAD_WIDTH : (k + 1) * HEAD_WIDTH]
        kvp[1, k] = vp[:, k * HEAD_WIDTH : (k + 1) * HEAD_WIDTH]
    for i, d in enumerate(order):
        for s in range(2):
            kpart[s, i] = kvp[s, kv_of((a + d) % half)]
    move_kv = send(kpart.at[1 - b], krx, ksem.at[2], ksem.at[3], mate())

    slot_ids = me * pages + lax.broadcasted_iota(jnp.int32, (pages, slots.shape[1]), 0)
    match = (slots[...] == slot_ids).astype(F32).astype(BF16)
    chosen = dot(match, selection[...].astype(F32).astype(BF16), ((1,), (1,)))
    spread_eye = (
        lax.broadcasted_iota(jnp.int32, (forks, both), 1) % forks
        == lax.broadcasted_iota(jnp.int32, (forks, both), 0)
    ).astype(F32)
    spread_bf = spread_eye.astype(BF16)
    selx[...] = dot(chosen.astype(BF16), spread_bf)

    get_q[0].wait()
    base = dot(h, wqbuf[0])
    for move in rank_moves:
        move.wait_recv()
    ranks = rtx[me]
    for o in range(1, n):
        ranks = ranks + rrx[o]
    ranks = ranks.astype(BF16).astype(F32)
    is_adapter = (
        lax.broadcasted_iota(jnp.int32, (ADAPTER_COUNT, forks), 0) == adapter[...]
    )
    rows = [
        jnp.where(is_adapter, ranks[r : r + 1], 0.0) for r in range(rank_local)
    ]
    spread = jnp.transpose(jnp.concatenate(rows, axis=0)).astype(BF16)

    moves1 = []
    for i, d in enumerate(order):
        if i:
            get_q[i].wait()
            base = dot(h, wqbuf[i])
        get_up[i].wait()
        total = base + dot(spread, upbuf[i].reshape(rank_local * ADAPTER_COUNT, wide))
        for s in range(2):
            part[i, s] = total[:, s * head_columns : (s + 1) * head_columns]
        moves1.append(send(part.at[i, 1 - b], rx1.at[i], s1.at[i], r1.at[i], mate()))
    get_wo = fetch(wo, wobuf)
    moves2 = []
    get_vc.wait()
    vtbuf[:, :, HEAD_WIDTH:, :] = jnp.ones(
        (pages, kv_local, vtbuf.shape[2] - HEAD_WIDTH, tokens), BF16
    )

    def turn(p, carry):
        for k in range(kv_local):
            block = vbuf[p, :, k * HEAD_WIDTH : (k + 1) * HEAD_WIDTH]
            vtbuf[p, k, :HEAD_WIDTH, :] = jnp.transpose(block)
        return carry

    for i, d in enumerate(order):
        lax.fori_loop(pages * i // half, pages * (i + 1) // half, turn, 0)
        if i == 0:
            move_kv.wait_recv()
        moves1[i].wait_recv()
        tx2[i, :, :head_columns] = part[i, b] + rx1[i]
        tx2[i, :, head_columns:] = kpart[b, i] + krx[i]
        if d:
            moves2.append(send(tx2.at[i], rx2.at[d], s2.at[d], r2.at[d], far(d)))
    merged = tx2[half - 1]
    for i, d in enumerate(order[:-1]):
        moves2[i].wait_recv()
        merged = merged + rx2[d]

    qfull[me] = merged[:, :head_columns].astype(BF16)
    kvx[b] = merged[:, head_columns:].astype(BF16)

    def gather(buf, ssem, rsem):
        near = send(buf.at[me], buf.at[me], ssem.at[0], rsem.at[0], mate())
        z = [
            send(buf.at[me], buf.at[me], ssem.at[d], rsem.at[d], far(d))
            for d in range(1, half)
        ]
        return near, z

    def forward(buf, ssem, rsem, z):
        passed = []
        for d in range(1, half):
            z[d - 1].wait_recv()
            slot = 2 * ((a + half - d) % half) + b
            passed.append(
                send(
                    buf.at[slot],
                    buf.at[slot],
                    ssem.at[half + d - 1],
                    rsem.at[half + d - 1],
                    mate(),
                )
            )
        return passed

    near, z = gather(qfull, gs, gr)
    kv_move = send(kvx.at[b], kvx.at[b], ksem.at[0], ksem.at[1], mate())

    batch = math.gcd(pages, 4)
    scale = HEAD_WIDTH ** (-0.5)
    scale2 = scale * math.log2(math.e)

    def attend(j, group):
        kv = kv_of(group)
        columns = pl.ds(pl.multiple_of(kv * HEAD_WIDTH, HEAD_WIDTH), HEAD_WIDTH)
        pieces = []
        for s in range(2):
            for t in range(per_owner):
                pieces.append(qfull[2 * group + s, :, t * HEAD_WIDTH : (t + 1) * HEAD_WIDTH])
        queries = jnp.concatenate(pieces, axis=0)
        acc[...] = jnp.zeros_like(acc)
        top0 = jnp.full((1, both), neg_floor, F32)
        mass0 = jnp.zeros((1, both), F32)

        def block(q, carry):
            top, mass = carry
            first = q * batch
            keys = kbuf[pl.ds(first, batch), :, columns].reshape(batch * tokens, HEAD_WIDTH)
            raw_all = dot(keys, queries, ((1,), (1,)))
            found = []
            new_top = top
            for u in range(batch):
                raw = raw_all[u * tokens : (u + 1) * tokens]
                peak = jnp.max(raw, axis=0, keepdims=True)
                probs = jnp.exp2((raw - peak) * scale2).astype(BF16)
                sums = dot(vtbuf[first + u, kv], probs)
                hit = selx[pl.ds(first + u, 1), :] > 0.5
                peak = jnp.where(hit, peak, neg_floor)
                new_top = jnp.maximum(new_top, peak)
                found.append((hit, peak, sums))
            keep = jnp.exp2((top - new_top) * scale2)
            mass = mass * keep
            total = acc[...] * keep
            for hit, peak, sums in found:
                fresh = jnp.where(hit, jnp.exp2((peak - new_top) * scale2), 0.0)
                total = total + sums[:HEAD_WIDTH] * fresh
                mass = mass + sums[HEAD_WIDTH : HEAD_WIDTH + 1] * fresh
            acc[...] = total
            return new_top, mass

        top, mass = lax.fori_loop(0, pages // batch, block, (top0, mass0))
        for s in range(2):
            part_lanes = slice(s * lanes, (s + 1) * lanes)
            resa[j, s] = acc[:, part_lanes].astype(BF16)
            ress[j, s, 0:1] = top[:, part_lanes]
            ress[j, s, 1:2] = mass[:, part_lanes]

    def join(items):
        top = items[0][1]
        for item in items[1:]:
            top = jnp.maximum(top, item[1])
        mass, total = 0.0, 0.0
        for x, t, w in items:
            factor = jnp.exp2((t - top) * scale2)
            mass = mass + w * factor
            total = total + x.astype(F32) * factor
        return total, top, mass

    moves3, moves4 = [], []

    def send_half(j):
        moves3.append(
            (
                send(resa.at[j, 1 - b], rxa.at[j], as1.at[j], ar1.at[j], mate()),
                send(ress.at[j, 1 - b], rxs.at[j], bs1.at[j], br1.at[j], mate()),
            )
        )

    def merge_half(j):
        for move in moves3[j]:
            move.wait_recv()
        total, top, mass = join(
            [
                (resa[j, b], ress[j, b, 0:1], ress[j, b, 1:2]),
                (rxa[j], rxs[j, 0:1], rxs[j, 1:2]),
            ]
        )
        if j == 0:
            return total, top, mass
        d = half - j
        txa[j] = total.astype(BF16)
        txs[j, 0:1] = top
        txs[j, 1:2] = mass
        moves4.append(
            (
                d,
                send(txa.at[j], fxa.at[d], as2.at[d], ar2.at[d], far(d)),
                send(txs.at[j], fxs.at[d], bs2.at[d], br2.at[d], far(d)),
            )
        )
        return None

    get_kc.wait()
    near.wait_recv()
    own_items = None
    passed = None
    for j in range(half):
        if j == 1:
            passed = forward(qfull, gs, gr, z)
        if j:
            passed[j - 1].wait_recv()
        attend(j, (a + half - j) % half)
        send_half(j)
        if j:
            result = merge_half(j - 1)
            if j == 1:
                own_items = result
    last = merge_half(half - 1)
    if half == 1:
        own_items = last

    kv_move.wait_recv()
    mine = jnp.concatenate(
        [qfull[me, :, t * HEAD_WIDTH : (t + 1) * HEAD_WIDTH] for t in range(per_owner)], axis=0
    )
    cross = dot(kvx[0], mine, ((1,), (1,)))
    own_eye = spread_eye[:, :lanes]
    own_score = jnp.sum(jnp.where(own_eye > 0.5, cross, 0.0), axis=0, keepdims=True)
    own_value = dot(kvx[1], own_eye.astype(BF16), ((0,), (0,)))
    items = [own_items, (own_value, own_score, jnp.ones((1, lanes), F32))]
    for d, move_a, move_s in moves4:
        move_a.wait_recv()
        move_s.wait_recv()
        items.append((fxa[d], fxs[d, 0:1], fxs[d, 1:2]))
    total, top, mass = join(items)
    context = jnp.transpose(total / mass)
    for t in range(per_owner):
        cfull[me, :, t * HEAD_WIDTH : (t + 1) * HEAD_WIDTH] = context[
            t * forks : (t + 1) * forks
        ].astype(BF16)

    near, z = gather(cfull, hs, hr)
    get_wo.wait()

    def project(slot):
        rows_ = pl.ds(pl.multiple_of(slot * head_columns, head_columns), head_columns)
        return dot(cfull[slot], wobuf[rows_, :])

    outp[...] = project(me)
    near.wait_recv()
    outp[...] += project(me + 1 - 2 * b)
    passed = forward(cfull, hs, hr, z)
    for d in range(1, half):
        outp[...] += project(2 * ((a + half - d) % half) + b)
    for d in range(1, half):
        passed[d - 1].wait_recv()
        outp[...] += project(2 * ((a + half - d) % half) + 1 - b)
    swap = send(outp, outr, osem.at[0], osem.at[1], {"tp": 1 - core})
    swap.wait_recv()
    out[...] = (outp[...] + outr[...]).astype(out.dtype)
    for copy in sends:
        copy.wait_send()


def shards(
    hidden,
    adapter,
    page_cache_slot,
    selection,
    query_projection_weight,
    key_projection_weight,
    value_projection_weight,
    adapter_down_weight,
    adapter_up_weight,
    output_projection_weight,
    prefix_key_cache,
    prefix_value_cache,
):
    n = lax.axis_size("mem")
    half = n // 2
    forks, depth = hidden.shape
    width = query_projection_weight.shape[1]
    kv_width = key_projection_weight.shape[1]
    kv_local = kv_width // HEAD_WIDTH
    group_size = width // kv_width
    columns = width // n
    lanes = (columns // HEAD_WIDTH) * forks
    out_width = output_projection_weight.shape[1]
    rank_local = adapter_up_weight.shape[0]
    pages, tokens = prefix_key_cache.shape[:2]
    down_width = adapter_down_weight.shape[1]
    chunks = 4
    dma = pltpu.SemaphoreType.DMA
    vmem = pltpu.VMEM
    scratch = [
        vmem((chunks, depth, down_width // chunks), BF16),
        vmem((2, depth, kv_width), BF16),
        vmem((half, depth, 2 * columns), BF16),
        vmem((half, rank_local, ADAPTER_COUNT, 2 * columns), BF16),
        vmem(prefix_key_cache.shape, BF16),
        vmem(prefix_value_cache.shape, BF16),
        vmem((pages, kv_local, HEAD_WIDTH + 16, tokens), BF16),
        vmem(output_projection_weight.shape, BF16),
        vmem((n, rank_local, forks), F32),
        vmem((n, rank_local, forks), F32),
        vmem((2, kv_local, forks, HEAD_WIDTH), F32),
        vmem((2, half, forks, HEAD_WIDTH), F32),
        vmem((half, forks, HEAD_WIDTH), F32),
        vmem((half, 2, forks, columns), F32),
        vmem((half, forks, columns), F32),
        vmem((half, forks, columns + HEAD_WIDTH), F32),
        vmem((half, forks, columns + HEAD_WIDTH), F32),
        vmem((n, forks, columns), BF16),
        vmem((2, forks, HEAD_WIDTH), BF16),
        vmem((pages, 2 * lanes), F32),
        vmem((HEAD_WIDTH, 2 * lanes), F32),
        vmem((half, 2, HEAD_WIDTH, lanes), BF16),
        vmem((half, 2, 2, lanes), F32),
        vmem((half, HEAD_WIDTH, lanes), BF16),
        vmem((half, 2, lanes), F32),
        vmem((half, HEAD_WIDTH, lanes), BF16),
        vmem((half, 2, lanes), F32),
        vmem((half, HEAD_WIDTH, lanes), BF16),
        vmem((half, 2, lanes), F32),
        vmem((n, forks, columns), BF16),
        vmem((forks, out_width), F32),
        vmem((forks, out_width), F32),
        dma((chunks + 2 + 2 * half + 3,)),
        dma((n,)),
        dma((n,)),
        dma((half,)),
        dma((half,)),
        dma((half,)),
        dma((half,)),
        dma((4,)),
        dma((n,)),
        dma((n,)),
        dma((n,)),
        dma((n,)),
        dma((half,)),
        dma((half,)),
        dma((half,)),
        dma((half,)),
        dma((half,)),
        dma((half,)),
        dma((half,)),
        dma((half,)),
        dma((2,)),
    ]
    small = pl.BlockSpec(memory_space=pltpu.VMEM)
    large = pl.BlockSpec(memory_space=pl.ANY)
    return pl.pallas_call(
        functools.partial(kernel, n, group_size),
        out_shape=jax.ShapeDtypeStruct((forks, out_width), BF16),
        in_specs=[small] * 4 + [large] * 8,
        out_specs=small,
        scratch_shapes=scratch,
        compiler_params=pltpu.CompilerParams(
            collective_id=0, has_side_effects=True, vmem_limit_bytes=60 * 1024 * 1024
        ),
    )(
        hidden,
        adapter.reshape(1, forks),
        page_cache_slot.reshape(1, page_cache_slot.shape[0]),
        selection,
        query_projection_weight,
        key_projection_weight,
        value_projection_weight,
        adapter_down_weight,
        adapter_up_weight,
        output_projection_weight,
        prefix_key_cache,
        prefix_value_cache,
    )


def solution(mesh):
    return jax.shard_map(
        shards,
        mesh=mesh,
        in_specs=(
            P("groups", "mem"),
            P("groups"),
            P("groups"),
            P("groups", None),
            P("mem", "tp"),
            P("mem", "tp"),
            P("mem", "tp"),
            P("mem", None),
            P("mem", None, "tp"),
            P("tp", "mem"),
            P(("groups", "mem"), None, "tp"),
            P(("groups", "mem"), None, "tp"),
        ),
        out_specs=P("groups", "mem"),
        check_vma=False,
    )
```

```python
import functools
import math

import jax
import jax.numpy as jnp
from jax import lax
from jax.experimental import pallas as pl
from jax.experimental.pallas import tpu as pltpu
from jax.sharding import PartitionSpec as P

HEAD_WIDTH = 128
ADAPTER_RANK = 64
ADAPTER_COUNT = 32
MESH = pl.DeviceIdType.MESH
F32 = jnp.float32
BF16 = jnp.bfloat16
neg_floor = -1e30
UNROLL = 1
BATCH = 8


def dot(x, y, dims=((1,), (0,))):
    return lax.dot_general(x, y, (dims, ((), ())), preferred_element_type=F32)


def kernel(
    n,
    group_size,
    hidden,
    adapter,
    slots,
    selection,
    wq,
    wk,
    wv,
    down,
    up,
    wo,
    kcache,
    vcache,
    out,
    dbuf,
    kvbuf,
    wqbuf,
    upbuf,
    kbuf,
    vbuf,
    vtbuf,
    wobuf,
    rtx,
    rrx,
    kvp,
    kpart,
    krx,
    tk2,
    rk2,
    part,
    rx1,
    tx2,
    rx2,
    qfull,
    kvx,
    selx,
    acc,
    resa,
    ress,
    rxa,
    rxs,
    txa,
    txs,
    fxa,
    fxs,
    cfull,
    outp,
    outr,
    loc,
    rsend,
    rrecv,
    s1,
    r1,
    s2,
    r2,
    ksem,
    ks2,
    kr2,
    gs,
    gr,
    hs,
    hr,
    as1,
    ar1,
    bs1,
    br1,
    as2,
    ar2,
    bs2,
    br2,
    osem,
):
    half = n // 2
    me = lax.axis_index("mem")
    core = lax.axis_index("tp")
    a = me // 2
    b = me % 2
    forks = hidden.shape[0]
    head_columns = wq.shape[1] // n
    per_owner = head_columns // HEAD_WIDTH
    wide = 2 * head_columns
    lanes = per_owner * forks
    both = 2 * lanes
    kv_local = wk.shape[1] // HEAD_WIDTH
    rank_local = up.shape[0]
    pages = kcache.shape[0]
    tokens = kcache.shape[1]
    sends = []

    def send(src, dst, ssem, rsem, where):
        copy = pltpu.make_async_remote_copy(
            src_ref=src,
            dst_ref=dst,
            send_sem=ssem,
            recv_sem=rsem,
            device_id=where,
            device_id_type=MESH,
        )
        copy.start()
        sends.append(copy)
        return copy

    def mate():
        return {"mem": me + 1 - 2 * b}

    def far(step):
        return {"mem": 2 * ((a + step) % half) + b}

    order = sorted(range(1, half), key=lambda d: -min(d, half - d)) + [0]
    locals_ = []

    def fetch(src, dst):
        copy = pltpu.make_async_copy(src, dst, loc.at[len(locals_)])
        copy.start()
        locals_.append(copy)
        return copy

    dchunks = dbuf.shape[0]
    dwide = dbuf.shape[2]
    get_down = [fetch(down.at[:, pl.ds(c * dwide, dwide)], dbuf.at[c]) for c in range(dchunks)]
    get_k = fetch(wk, kvbuf.at[0])
    get_v = fetch(wv, kvbuf.at[1])
    get_q, get_up = [], []

    def fetch_piece(i):
        columns = pl.ds(pl.multiple_of(((a + order[i]) % half) * wide, wide), wide)
        get_q.append(fetch(wq.at[:, columns], wqbuf.at[i]))
        get_up.append(fetch(up.at[:, :, columns], upbuf.at[i]))

    fetch_piece(0)

    barrier = pltpu.get_barrier_semaphore()
    for o in range(1, n):
        pl.semaphore_signal(barrier, inc=1, device_id={"mem": (me + o) % n}, device_id_type=MESH)
    pl.semaphore_signal(barrier, inc=1, device_id={"tp": 1 - core}, device_id_type=MESH)

    h = hidden[...]
    ids = adapter[...].astype(F32)
    eye = lax.broadcasted_iota(jnp.int32, (forks, forks), 0) == lax.broadcasted_iota(
        jnp.int32, (forks, forks), 1
    )
    id_column = jnp.sum(jnp.where(eye, ids, 0.0), axis=1, keepdims=True)
    per_tile = 128 // ADAPTER_RANK
    lane_part = (
        lax.broadcasted_iota(jnp.int32, (forks, 128), 1) // ADAPTER_RANK
    ).astype(F32)
    folded = jnp.zeros((forks, 128), F32)
    for c in range(dchunks):
        get_down[c].wait()
        act = dot(h, dbuf[c])
        for t in range(dwide // 128):
            first = (c * (dwide // 128) + t) * per_tile
            folded += jnp.where(
                id_column - float(first) == lane_part, act[:, t * 128 : (t + 1) * 128], 0.0
            )
    for i in range(1, half):
        fetch_piece(i)
    turned = jnp.transpose(folded)
    rank_part = turned[:ADAPTER_RANK]
    for t in range(1, per_tile):
        rank_part += turned[t * ADAPTER_RANK : (t + 1) * ADAPTER_RANK]
    for j in range(n):
        rtx[j] = rank_part[j * rank_local : (j + 1) * rank_local]
    pl.semaphore_wait(barrier, n)
    rank_moves = []
    for o in range(1, n):
        to = (me + o) % n
        rank_moves.append(
            send(rtx.at[to], rrx.at[o], rsend.at[o], rrecv.at[o], {"mem": to})
        )

    def kv_of(group):
        return (group * 2 * per_owner) // group_size

    get_k.wait()
    kp = dot(h, kvbuf[0])
    get_v.wait()
    vp = dot(h, kvbuf[1])
    get_vc = fetch(vcache, vbuf)
    get_kc = fetch(kcache, kbuf)
    for k in range(kv_local):
        kvp[0, k] = kp[:, k * HEAD_WIDTH : (k + 1) * HEAD_WIDTH]
        kvp[1, k] = vp[:, k * HEAD_WIDTH : (k + 1) * HEAD_WIDTH]
    for i, d in enumerate(order):
        for s in range(2):
            kpart[s, i] = kvp[s, kv_of((a + d) % half)]
    move_kv = send(kpart.at[1 - b], krx, ksem.at[2], ksem.at[3], mate())

    slot_ids = me * pages + lax.broadcasted_iota(jnp.int32, (pages, slots.shape[1]), 0)
    match = (slots[...] == slot_ids).astype(F32).astype(BF16)
    chosen = dot(match, selection[...].astype(F32).astype(BF16), ((1,), (1,)))
    spread_eye = (
        lax.broadcasted_iota(jnp.int32, (forks, both), 1) % forks
        == lax.broadcasted_iota(jnp.int32, (forks, both), 0)
    ).astype(F32)
    spread_bf = spread_eye.astype(BF16)
    selx[...] = dot(chosen.astype(BF16), spread_bf)

    get_q[0].wait()
    base = dot(h, wqbuf[0])
    for move in rank_moves:
        move.wait_recv()
    ranks = rtx[me]
    for o in range(1, n):
        ranks = ranks + rrx[o]
    ranks = ranks.astype(BF16).astype(F32)
    is_adapter = (
        lax.broadcasted_iota(jnp.int32, (ADAPTER_COUNT, forks), 0) == adapter[...]
    )
    rows = [
        jnp.where(is_adapter, ranks[r : r + 1], 0.0) for r in range(rank_local)
    ]
    spread = jnp.transpose(jnp.concatenate(rows, axis=0)).astype(BF16)

    moves1 = []
    for i, d in enumerate(order):
        if i:
            get_q[i].wait()
            base = dot(h, wqbuf[i])
        get_up[i].wait()
        total = base + dot(spread, upbuf[i].reshape(rank_local * ADAPTER_COUNT, wide))
        for s in range(2):
            part[i, s] = total[:, s * head_columns : (s + 1) * head_columns]
        moves1.append(send(part.at[i, 1 - b], rx1.at[i], s1.at[i], r1.at[i], mate()))
        if i == 0:
            move_kv.wait_recv()
            moves_kv = []
            for e, step in enumerate(order):
                tk2[e] = kpart[b, e] + krx[e]
                if step:
                    moves_kv.append(
                        send(tk2.at[e], rk2.at[step], ks2.at[step], kr2.at[step], far(step))
                    )
    get_wo = fetch(wo, wobuf)
    moves2 = []
    get_vc.wait()
    vtbuf[:, :, HEAD_WIDTH:, :] = jnp.ones(
        (pages, kv_local, vtbuf.shape[2] - HEAD_WIDTH, tokens), BF16
    )

    def turn(p, carry):
        for k in range(kv_local):
            block = vbuf[p, :, k * HEAD_WIDTH : (k + 1) * HEAD_WIDTH]
            vtbuf[p, k, :HEAD_WIDTH, :] = jnp.transpose(block)
        return carry

    for i, d in enumerate(order):
        lax.fori_loop(pages * i // half, pages * (i + 1) // half, turn, 0)
        moves1[i].wait_recv()
        tx2[i] = part[i, b] + rx1[i]
        if d:
            moves2.append(send(tx2.at[i], rx2.at[d], s2.at[d], r2.at[d], far(d)))
    merged = tx2[half - 1]
    for i, d in enumerate(order[:-1]):
        moves2[i].wait_recv()
        merged = merged + rx2[d]
    merged_kv = tk2[half - 1]
    for i, d in enumerate(order[:-1]):
        moves_kv[i].wait_recv()
        merged_kv = merged_kv + rk2[d]

    qfull[me] = merged.astype(BF16)
    kvx[b] = merged_kv.astype(BF16)

    def gather(buf, ssem, rsem):
        near = send(buf.at[me], buf.at[me], ssem.at[0], rsem.at[0], mate())
        z = [
            send(buf.at[me], buf.at[me], ssem.at[d], rsem.at[d], far(d))
            for d in range(1, half)
        ]
        return near, z

    def forward(buf, ssem, rsem, z, steps):
        passed = []
        for d in steps:
            z[d - 1].wait_recv()
            slot = 2 * ((a + half - d) % half) + b
            passed.append(
                send(
                    buf.at[slot],
                    buf.at[slot],
                    ssem.at[half + d - 1],
                    rsem.at[half + d - 1],
                    mate(),
                )
            )
        return passed

    near, z = gather(qfull, gs, gr)
    kv_move = send(kvx.at[b], kvx.at[b], ksem.at[0], ksem.at[1], mate())

    batch = math.gcd(pages, BATCH)
    scale = HEAD_WIDTH ** (-0.5)
    scale2 = scale * math.log2(math.e)

    def attend(j, group):
        kv = kv_of(group)
        columns = pl.ds(pl.multiple_of(kv * HEAD_WIDTH, HEAD_WIDTH), HEAD_WIDTH)
        pieces = []
        for s in range(2):
            for t in range(per_owner):
                pieces.append(qfull[2 * group + s, :, t * HEAD_WIDTH : (t + 1) * HEAD_WIDTH])
        queries = jnp.concatenate(pieces, axis=0)
        acc[...] = jnp.zeros_like(acc)
        top0 = jnp.full((1, both), neg_floor, F32)
        mass0 = jnp.zeros((1, both), F32)

        def block(q, carry):
            top, mass = carry
            first = q * batch
            keys = kbuf[pl.ds(first, batch), :, columns].reshape(batch * tokens, HEAD_WIDTH)
            raw_all = dot(keys, queries, ((1,), (1,)))
            found = []
            new_top = top
            for u in range(batch):
                raw = raw_all[u * tokens : (u + 1) * tokens]
                peak = jnp.max(raw, axis=0, keepdims=True)
                probs = jnp.exp2((raw - peak) * scale2).astype(BF16)
                sums = dot(vtbuf[first + u, kv], probs)
                hit = selx[pl.ds(first + u, 1), :] > 0.5
                peak = jnp.where(hit, peak, neg_floor)
                new_top = jnp.maximum(new_top, peak)
                found.append((hit, peak, sums))
            keep = jnp.exp2((top - new_top) * scale2)
            mass = mass * keep
            total = acc[...] * keep
            for hit, peak, sums in found:
                fresh = jnp.where(hit, jnp.exp2((peak - new_top) * scale2), 0.0)
                total = total + sums[:HEAD_WIDTH] * fresh
                mass = mass + sums[HEAD_WIDTH : HEAD_WIDTH + 1] * fresh
            acc[...] = total
            return new_top, mass

        blocks = pages // batch
        state = lax.fori_loop(0, blocks // 2, block, (top0, mass0), unroll=UNROLL)
        if j == 0 and half > 1:
            passed.extend(forward(qfull, gs, gr, z, [1]))
        top, mass = lax.fori_loop(blocks // 2, blocks, block, state, unroll=UNROLL)
        for s in range(2):
            part_lanes = slice(s * lanes, (s + 1) * lanes)
            resa[j, s] = acc[:, part_lanes].astype(BF16)
            ress[j, s, 0:1] = top[:, part_lanes]
            ress[j, s, 1:2] = mass[:, part_lanes]

    def join(items):
        top = items[0][1]
        for item in items[1:]:
            top = jnp.maximum(top, item[1])
        mass, total = 0.0, 0.0
        for x, t, w in items:
            factor = jnp.exp2((t - top) * scale2)
            mass = mass + w * factor
            total = total + x.astype(F32) * factor
        return total, top, mass

    moves3, moves4 = [], []

    def send_half(j):
        moves3.append(
            (
                send(resa.at[j, 1 - b], rxa.at[j], as1.at[j], ar1.at[j], mate()),
                send(ress.at[j, 1 - b], rxs.at[j], bs1.at[j], br1.at[j], mate()),
            )
        )

    def merge_half(j):
        for move in moves3[j]:
            move.wait_recv()
        total, top, mass = join(
            [
                (resa[j, b], ress[j, b, 0:1], ress[j, b, 1:2]),
                (rxa[j], rxs[j, 0:1], rxs[j, 1:2]),
            ]
        )
        if j == 0:
            return total, top, mass
        d = half - j
        txa[j] = total.astype(BF16)
        txs[j, 0:1] = top
        txs[j, 1:2] = mass
        moves4.append(
            (
                d,
                send(txa.at[j], fxa.at[d], as2.at[d], ar2.at[d], far(d)),
                send(txs.at[j], fxs.at[d], bs2.at[d], br2.at[d], far(d)),
            )
        )
        return None

    get_kc.wait()
    near.wait_recv()
    own_items = None
    passed = []
    for j in range(half):
        if j == 1:
            passed += forward(qfull, gs, gr, z, range(2, half))
        if j:
            passed[j - 1].wait_recv()
        attend(j, (a + half - j) % half)
        send_half(j)
        if j:
            result = merge_half(j - 1)
            if j == 1:
                own_items = result
    last = merge_half(half - 1)
    if half == 1:
        own_items = last

    kv_move.wait_recv()
    mine = jnp.concatenate(
        [qfull[me, :, t * HEAD_WIDTH : (t + 1) * HEAD_WIDTH] for t in range(per_owner)], axis=0
    )
    cross = dot(kvx[0], mine, ((1,), (1,)))
    own_eye = spread_eye[:, :lanes]
    own_score = jnp.sum(jnp.where(own_eye > 0.5, cross, 0.0), axis=0, keepdims=True)
    own_value = dot(kvx[1], own_eye.astype(BF16), ((0,), (0,)))
    items = [own_items, (own_value, own_score, jnp.ones((1, lanes), F32))]
    for d, move_a, move_s in moves4:
        move_a.wait_recv()
        move_s.wait_recv()
        items.append((fxa[d], fxs[d, 0:1], fxs[d, 1:2]))
    total, top, mass = join(items)
    context = jnp.transpose(total / mass)
    for t in range(per_owner):
        cfull[me, :, t * HEAD_WIDTH : (t + 1) * HEAD_WIDTH] = context[
            t * forks : (t + 1) * forks
        ].astype(BF16)

    near, z = gather(cfull, hs, hr)
    get_wo.wait()

    def project(slot):
        rows_ = pl.ds(pl.multiple_of(slot * head_columns, head_columns), head_columns)
        return dot(cfull[slot], wobuf[rows_, :])

    outp[...] = project(me)
    near.wait_recv()
    outp[...] += project(me + 1 - 2 * b)
    passed = forward(cfull, hs, hr, z, range(1, half))
    for d in range(1, half):
        outp[...] += project(2 * ((a + half - d) % half) + b)
    for d in range(1, half):
        passed[d - 1].wait_recv()
        outp[...] += project(2 * ((a + half - d) % half) + 1 - b)
    swap = send(outp, outr, osem.at[0], osem.at[1], {"tp": 1 - core})
    swap.wait_recv()
    out[...] = (outp[...] + outr[...]).astype(out.dtype)
    for copy in sends:
        copy.wait_send()


def shards(
    hidden,
    adapter,
    page_cache_slot,
    selection,
    query_projection_weight,
    key_projection_weight,
    value_projection_weight,
    adapter_down_weight,
    adapter_up_weight,
    output_projection_weight,
    prefix_key_cache,
    prefix_value_cache,
):
    n = lax.axis_size("mem")
    half = n // 2
    forks, depth = hidden.shape
    width = query_projection_weight.shape[1]
    kv_width = key_projection_weight.shape[1]
    kv_local = kv_width // HEAD_WIDTH
    group_size = width // kv_width
    columns = width // n
    lanes = (columns // HEAD_WIDTH) * forks
    out_width = output_projection_weight.shape[1]
    rank_local = adapter_up_weight.shape[0]
    pages, tokens = prefix_key_cache.shape[:2]
    down_width = adapter_down_weight.shape[1]
    chunks = 4
    dma = pltpu.SemaphoreType.DMA
    vmem = pltpu.VMEM
    scratch = [
        vmem((chunks, depth, down_width // chunks), BF16),
        vmem((2, depth, kv_width), BF16),
        vmem((half, depth, 2 * columns), BF16),
        vmem((half, rank_local, ADAPTER_COUNT, 2 * columns), BF16),
        vmem(prefix_key_cache.shape, BF16),
        vmem(prefix_value_cache.shape, BF16),
        vmem((pages, kv_local, HEAD_WIDTH + 16, tokens), BF16),
        vmem(output_projection_weight.shape, BF16),
        vmem((n, rank_local, forks), F32),
        vmem((n, rank_local, forks), F32),
        vmem((2, kv_local, forks, HEAD_WIDTH), F32),
        vmem((2, half, forks, HEAD_WIDTH), F32),
        vmem((half, forks, HEAD_WIDTH), F32),
        vmem((half, forks, HEAD_WIDTH), F32),
        vmem((half, forks, HEAD_WIDTH), F32),
        vmem((half, 2, forks, columns), F32),
        vmem((half, forks, columns), F32),
        vmem((half, forks, columns), F32),
        vmem((half, forks, columns), F32),
        vmem((n, forks, columns), BF16),
        vmem((2, forks, HEAD_WIDTH), BF16),
        vmem((pages, 2 * lanes), F32),
        vmem((HEAD_WIDTH, 2 * lanes), F32),
        vmem((half, 2, HEAD_WIDTH, lanes), BF16),
        vmem((half, 2, 2, lanes), F32),
        vmem((half, HEAD_WIDTH, lanes), BF16),
        vmem((half, 2, lanes), F32),
        vmem((half, HEAD_WIDTH, lanes), BF16),
        vmem((half, 2, lanes), F32),
        vmem((half, HEAD_WIDTH, lanes), BF16),
        vmem((half, 2, lanes), F32),
        vmem((n, forks, columns), BF16),
        vmem((forks, out_width), F32),
        vmem((forks, out_width), F32),
        dma((chunks + 2 + 2 * half + 3,)),
        dma((n,)),
        dma((n,)),
        dma((half,)),
        dma((half,)),
        dma((half,)),
        dma((half,)),
        dma((4,)),
        dma((half,)),
        dma((half,)),
        dma((n,)),
        dma((n,)),
        dma((n,)),
        dma((n,)),
        dma((half,)),
        dma((half,)),
        dma((half,)),
        dma((half,)),
        dma((half,)),
        dma((half,)),
        dma((half,)),
        dma((half,)),
        dma((2,)),
    ]
    small = pl.BlockSpec(memory_space=pltpu.VMEM)
    large = pl.BlockSpec(memory_space=pl.ANY)
    return pl.pallas_call(
        functools.partial(kernel, n, group_size),
        out_shape=jax.ShapeDtypeStruct((forks, out_width), BF16),
        in_specs=[small] * 4 + [large] * 8,
        out_specs=small,
        scratch_shapes=scratch,
        compiler_params=pltpu.CompilerParams(
            collective_id=0, has_side_effects=True, vmem_limit_bytes=60 * 1024 * 1024
        ),
    )(
        hidden,
        adapter.reshape(1, forks),
        page_cache_slot.reshape(1, page_cache_slot.shape[0]),
        selection,
        query_projection_weight,
        key_projection_weight,
        value_projection_weight,
        adapter_down_weight,
        adapter_up_weight,
        output_projection_weight,
        prefix_key_cache,
        prefix_value_cache,
    )


def solution(mesh):
    return jax.shard_map(
        shards,
        mesh=mesh,
        in_specs=(
            P("groups", "mem"),
            P("groups"),
            P("groups"),
            P("groups", None),
            P("mem", "tp"),
            P("mem", "tp"),
            P("mem", "tp"),
            P("mem", None),
            P("mem", None, "tp"),
            P("tp", "mem"),
            P(("groups", "mem"), None, "tp"),
            P(("groups", "mem"), None, "tp"),
        ),
        out_specs=P("groups", "mem"),
        check_vma=False,
    )
```
